512 devices in a mesh: dp: 32 (over x, y), expert: 16 (over z, core).
Axes of the slice: x: 4, y: 8, z: 8, core: 2. Of those that a mesh axis runs over, the one named last changes fastest.
Arguments:
- tokens: bfloat16 [8192, 2048], P('expert', 'dp'), may hold values from -6 to 6
- routes: int32 [8192, 2], P('expert'), may hold values from 0 to 15, all different within a row; in each aligned block of 512 rows (0 to 511, 512 to 1023, ...) at most 96 rows name the same one
- scores: int32 [8192, 2], P('expert'), may hold values from 1 to 1023
- gate_weight: bfloat16 [16, 2048, 8192], P('expert', None, 'dp'), may hold values from -0.125 to 0.125
- up_weight: bfloat16 [16, 2048, 8192], P('expert', None, 'dp'), may hold values from -0.125 to 0.125
- down_weight: bfloat16 [16, 8192, 2048], P('expert', 'dp'), may hold values from -0.0625 to 0.0625
Outputs:
- layer_out: bfloat16 [8192, 2048], P('expert', 'dp')
The draws below stay inside these ranges and needn't reach their ends.
Inputs may be any that keep to these rules, and one draw needn't show every extreme that they name: `routes`: each row names 2 different experts. Within each aligned block of 512 rows no expert is named by more than 96 rows, and in every draw some expert is named by exactly 96 rows of a block.
All inputs are finite; a program needn't handle non-finite values.
Results may differ from the reference program's by a relative error of at most 0.025.
Values may be sent and summed in bfloat16 or wider, within the bound.
A program may use at most 64 MiB of HBM per device.

```python
import math
import jax
import jax.numpy as jnp
import numpy as np
from jax import lax

D = 2048
FF = 8192
TOP = 2
TOK_E = 512
EXPERTS = 16
CAP = 96
TOKENS = 8192
N_DP = 32
N_EXPERT = 16


def place_ends(values, stream_key, smallest, largest):
    extent = values.shape
    index_at = [jax.random.randint(jax.random.fold_in(stream_key, axis), (), 0, extent[axis]) for axis in range(len(extent))]
    values = values.at[tuple(index_at)].set(smallest)
    longest = extent.index(max(extent))
    index_at[longest] = (index_at[longest] + 1) % extent[longest]
    return values.at[tuple(index_at)].set(largest)


def level_of(key, shape, pieces, least, largest):
    gain, own = 1.0, jax.random.fold_in(key, 6)
    for axis_at, parts in pieces:
        heights = jnp.exp(jax.random.uniform(jax.random.fold_in(own, axis_at), (parts,), jnp.float32, least / len(pieces), largest / len(pieces)))
        gain = gain * jnp.repeat(heights, shape[axis_at] // parts).reshape([-1 if axis == axis_at else 1 for axis in range(len(shape))])
    return gain


def routed_block(stream_key, own, number, rows, amount, top, bound, lean):
    sequence = jax.random.permutation(stream_key, amount)
    crowded, common = shares(amount, rows * top, bound, lean, True), shares(amount, rows * top, bound, lean, False)
    places = jnp.arange(amount)

    def named(sizes, offset_by):
        used = int((sizes > 0).sum())
        fixed = max(1, used // 4)
        shifted = fixed + (places - fixed + offset_by * (used - fixed)) % max(1, amount - fixed)
        return jnp.zeros((amount,), jnp.int32).at[sequence[jnp.where(places < fixed, places, shifted)]].set(jnp.asarray(sizes, jnp.int32))

    sizes = jnp.where(number % 4 == 0, named(crowded, number // 4), named(common, number - number // 4 - 1))
    mixed = jax.random.permutation(jax.random.fold_in(own, 3), amount)
    donor, receiver = mixed[0:amount // 2 * 2:2], mixed[1:amount // 2 * 2:2]
    margin = jnp.minimum(sizes[donor] - 1, bound - sizes[receiver]) // 2
    margin = jnp.where((donor == sequence[0]) | (receiver == sequence[0]) | (sizes[receiver] == 0), 0, jnp.maximum(margin, 0))
    shifted = jax.random.randint(jax.random.fold_in(own, 4), (amount // 2,), 0, 1 << 20) % (margin + 1)
    sizes = sizes.at[donor].add(-shifted).at[receiver].add(shifted)
    items = jnp.searchsorted(jnp.cumsum(sizes), jnp.arange(rows * top), side="right").astype(jnp.int32)
    grid = items.reshape(top, rows).T
    grid = grid[jax.random.permutation(jax.random.fold_in(own, 1), rows)]
    offset_by = jax.random.randint(jax.random.fold_in(own, 2), (rows, 1), 0, top)
    return jnp.take_along_axis(grid, (jnp.arange(top)[None, :] + offset_by) % top, axis=1)


def shares(number_of, total, most, skew, full):
    loads = [(1 << 20) // math.isqrt(grade ** skew) + 1 for grade in range(1, number_of + 1)]
    largest = most if full else min(most, max(-(-total // number_of), total * loads[0] // sum(loads)))
    least = 1 if total - largest >= number_of - 1 else 0
    holding, surplus = [largest] + [least] * (number_of - 1), total - largest - least * (number_of - 1)
    while surplus > 0:
        candidates = [i for i in range(1, number_of) if holding[i] < largest] or [i for i in range(1, number_of) if holding[i] < most]
        pool, left = sum([loads[i] for i in candidates]), surplus
        for i in candidates:
            more = min(most - holding[i], max(1, left * loads[i] // pool), surplus)
            holding[i] = holding[i] + more
            surplus = surplus - more
    return np.array(holding)


def noise(key, dims, scale, bound, cuts=(), kind=jnp.bfloat16):
    gain = level_of(key, dims, cuts, -0.22, 0.18) if cuts else 1.0
    result = jax.random.normal(key, dims, jnp.float32) * scale * gain
    return jnp.minimum(jnp.maximum(result, -bound), bound).astype(kind)


def setup_inputs(seed: int = 0) -> dict:
    seeds = jax.random.split(jax.random.key(seed), 7)
    tokens = noise(seeds[0], (TOKENS, D), 1.0, 6.0, ((0, 16), (1, 32)))
    routes_keys = jax.random.split(jax.random.fold_in(seeds[1], 1), TOKENS // TOK_E)
    routes_turns = jax.random.permutation(jax.random.fold_in(seeds[1], 3), TOKENS // TOK_E)
    routes = jax.vmap(lambda own, number: routed_block(jax.random.fold_in(seeds[1], 2), own, number, TOK_E, EXPERTS, TOP, CAP, 2))(routes_keys, routes_turns).reshape((TOKENS, TOP))
    scores = place_ends(jax.random.randint(seeds[2], (TOKENS, TOP), 1, 1024), jax.random.fold_in(seeds[2], 1), 1, 1023).astype(jnp.int32)
    gate_weight = noise(seeds[3], (EXPERTS, D, FF), D ** -0.5, 0.125, ((0, 16), (2, 32)))
    up_weight = noise(seeds[4], (EXPERTS, D, FF), D ** -0.5, 0.125, ((0, 16), (2, 32)))
    down_weight = noise(seeds[5], (EXPERTS, FF, D), FF ** -0.5, 0.0625, ((0, 16), (1, 32)))
    return {"tokens": tokens, "routes": routes, "scores": scores, "gate_weight": gate_weight, "up_weight": up_weight, "down_weight": down_weight}


def reference(tokens, routes, scores, gate_weight, up_weight, down_weight):
    row_count = tokens.shape[0]
    expert_count = gate_weight.shape[0]
    slot_count = N_EXPERT * CAP
    block_cols = FF // N_DP
    flat_routes = routes.reshape(-1)
    onehot = (flat_routes[:, None] == jnp.arange(expert_count, dtype=jnp.int32)[None, :]).astype(jnp.int32)
    earlier = jnp.cumsum(onehot, axis=0) - onehot
    slot_rank = jnp.sum(onehot * earlier, axis=1).astype(jnp.int32)
    row_ids = jnp.repeat(jnp.arange(row_count, dtype=jnp.int32), TOP)
    row_table = jnp.zeros((expert_count, slot_count), jnp.int32).at[flat_routes, slot_rank].set(row_ids)

    def expert_result(packed):
        row_index, gate_mat, up_mat, down_mat = packed
        gathered = tokens[row_index]
        gate = jnp.dot(gathered, gate_mat, preferred_element_type=jnp.float32)
        upval = jnp.dot(gathered, up_mat, preferred_element_type=jnp.float32)
        hidden = (jax.nn.silu(gate) * upval).astype(jnp.bfloat16)

        def add_block(block, total):
            start = (block * block_cols).astype(jnp.int32)
            hidden_block = lax.dynamic_slice_in_dim(hidden, start, block_cols, 1)
            down_block = lax.dynamic_slice_in_dim(down_mat, start, block_cols, 0)
            rounded = lax.optimization_barrier(jnp.dot(hidden_block, down_block, preferred_element_type=jnp.float32).astype(jnp.bfloat16))
            return total + rounded.astype(jnp.float32)

        return lax.fori_loop(0, N_DP, add_block, jnp.zeros((slot_count, D), jnp.float32))

    results = lax.map(expert_result, (row_table, gate_weight, up_weight, down_weight))
    picked = results[flat_routes, slot_rank].reshape(row_count, TOP, D)
    weight = scores.astype(jnp.float32)
    weight = weight / jnp.sum(weight, axis=1, keepdims=True)
    combined = jnp.sum(weight[:, :, None] * picked, axis=1)
    return combined.astype(jnp.bfloat16)
```

```python
import functools

import jax
import jax.numpy as jnp
from jax import lax
from jax.experimental import pallas as pl
from jax.experimental.pallas import tpu as pltpu
from jax.sharding import PartitionSpec as P

MESH = pl.DeviceIdType.MESH
NX, NY = 4, 8
LANES = 128
BF, F32 = jnp.bfloat16, jnp.float32


def moe_kernel(
    tokens_ref, routes_ref, scores_ref, gate_hbm, up_hbm, down_hbm, out_ref,
    gate_raw, up_raw, down_raw, gu_t, down_t, sel, disp_out, disp_in,
    x_buf, acc, hid, o_buf, r_main, r_turn, ret_out, ret_in, pick0, pick1,
    load_sem, disp_send, disp_recv, ag_send, ag_recv, rs_send, rs_recv, turn_recv, ret_send, ret_recv,
):
    n_exp = disp_in.shape[0]
    rows, width = tokens_ref.shape
    group = n_exp // 4
    span = x_buf.shape[3]
    cap = span // group
    hidden = gate_raw.shape[3]
    dp = lax.axis_index("dp")
    me = lax.axis_index("expert")
    x, y = dp // NY, dp % NY

    def at_xy(px, py):
        return (lax.rem(px + NX, NX) * NY + lax.rem(py + NY, NY), me)

    loads = [
        pltpu.make_async_copy(src, dst, load_sem.at[i])
        for i, (src, dst) in enumerate(((gate_hbm, gate_raw), (up_hbm, up_raw), (down_hbm, down_raw)))
    ]
    for load in loads:
        load.start()

    barrier = pltpu.get_barrier_semaphore()
    for target in (at_xy(x + 1, y), at_xy(x - 1, y), at_xy(x, y + 1), at_xy(x, y - 1)):
        pl.semaphore_signal(barrier, inc=1, device_id=target, device_id_type=MESH)
    for p in range(1, n_exp):
        pl.semaphore_signal(barrier, inc=1, device_id=(dp, lax.rem(me + p, n_exp)), device_id_type=MESH)

    routes = routes_ref[...]
    first, second = routes[:, 0:1], routes[:, 1:2]
    lane = lax.broadcasted_iota(jnp.int32, (rows, LANES), 1)
    is_first = (lane == first).astype(F32)
    is_second = (lane == second).astype(F32)
    earlier_mask = (
        lax.broadcasted_iota(jnp.int32, (rows, rows), 1) < lax.broadcasted_iota(jnp.int32, (rows, rows), 0)
    ).astype(F32).astype(BF)
    earlier = jnp.dot(earlier_mask, (is_first + is_second).astype(BF), preferred_element_type=F32)
    rank0 = jnp.sum(is_first * earlier, axis=1, keepdims=True).astype(jnp.int32)
    rank1 = jnp.sum(is_second * earlier, axis=1, keepdims=True).astype(jnp.int32)
    slot0 = first * LANES + rank0
    slot1 = second * LANES + rank1

    tok = tokens_ref[...]
    wide = group * LANES
    for q in range(4):
        ids = lax.broadcasted_iota(jnp.int32, (rows, wide), 1) + q * wide
        p0 = (ids == slot0).astype(F32)
        p1 = (ids == slot1).astype(F32)
        pick0[:, q * wide:(q + 1) * wide] = p0.astype(BF)
        pick1[:, q * wide:(q + 1) * wide] = p1.astype(BF)
        packed = lax.dot_general(
            tok, (p0 + p1).astype(BF), (((0,), (0,)), ((), ())), preferred_element_type=F32
        ).astype(BF)
        for i in range(group):
            disp_out[q * group + i] = packed[:, i * LANES:(i + 1) * LANES]
    disp_in[me] = disp_out[me]

    pl.semaphore_wait(barrier, 4 + n_exp - 1)

    def disp_copy(dest, src):
        return pltpu.make_async_remote_copy(
            src_ref=disp_out.at[dest], dst_ref=disp_in.at[src], send_sem=disp_send, recv_sem=disp_recv.at[src],
            device_id=(dp, dest), device_id_type=MESH)

    for p in range(1, n_exp):
        disp_copy(lax.rem(me + p, n_exp), me).start()

    si = lax.broadcasted_iota(jnp.int32, (wide, span), 0)
    sl = lax.broadcasted_iota(jnp.int32, (wide, span), 1)
    rank_in = si % LANES
    sel[...] = ((sl == (si // LANES) * cap + rank_in) & (rank_in < cap)).astype(F32).astype(BF)

    for st in range(4):
        acc[st] = jnp.zeros(acc.shape[1:], F32)

    for load in loads:
        load.wait()

    @pl.loop(0, NY)
    def _(yy):
        g = gate_raw[:, yy].reshape(NX * width, hidden)
        u = up_raw[:, yy].reshape(NX * width, hidden)
        gu_t[yy, 0:hidden, :] = g.T
        gu_t[yy, hidden:2 * hidden, :] = u.T

    for c in range(NX * NY // 2):
        turned = down_raw[:, c * LANES:(c + 1) * LANES].T
        for h in range(2):
            xx, yy = (2 * c + h) // NY, (2 * c + h) % NY
            down_t[yy, xx * width:(xx + 1) * width, :] = turned[h * width:(h + 1) * width, :]

    streams = [(True, 1), (True, -1), (False, 1), (False, -1)]

    def where(sign, j, k):
        px = lax.rem(x - sign * j + 2 * NX, NX)
        py = lax.rem(y - sign * k + 2 * NY, NY)
        return px, py

    def piece(buf, st, sign, j, k):
        px, py = where(sign, j, k)
        return buf.at[st, py, pl.ds(pl.multiple_of(px * width, width), width)]

    def ag_copy(st, sign, j, k, along_x):
        ref = piece(x_buf, st, sign, j, k)
        return pltpu.make_async_remote_copy(
            src_ref=ref, dst_ref=ref, send_sem=ag_send.at[st],
            recv_sem=ag_recv.at[st, j + 1, k] if along_x else ag_recv.at[st, j, k + 1],
            device_id=at_xy(x + sign, y) if along_x else at_xy(x, y + sign), device_id_type=MESH)

    def ag_wait(st, sign, j, k):
        ref = piece(x_buf, st, sign, j, k)
        pltpu.make_async_copy(ref, ref, ag_recv.at[st, j, k]).wait()

    for st, (y_first, sign) in enumerate(streams):
        for s in range(st * group, (st + 1) * group):
            @pl.when(s != me)
            def _():
                pltpu.make_async_copy(disp_in.at[s], disp_in.at[s], disp_recv.at[s]).wait()
        packed = jnp.concatenate([disp_in[st * group + i] for i in range(group)], axis=1)
        x_buf[st, y, pl.ds(pl.multiple_of(x * width, width), width), :] = jnp.dot(
            packed, sel[...], preferred_element_type=F32).astype(BF)
        ag_copy(st, sign, 0, 0, True).start()
        ag_copy(st, sign, 0, 0, False).start()

    @pl.loop(1, NX + NY - 1)
    def _(r):
        for j in range(NX):
            k = r - j

            @pl.when((k >= 0) & (k < NY))
            def _():
                for st, (y_first, sign) in enumerate(streams):
                    ag_wait(st, sign, j, k)
                    if y_first:
                        if j < NX - 1:
                            ag_copy(st, sign, j, k, True).start()
                        if j == 0:
                            @pl.when(k < NY - 1)
                            def _():
                                ag_copy(st, sign, j, k, False).start()
                    else:
                        if j < NX - 1:
                            @pl.when(k == 0)
                            def _():
                                ag_copy(st, sign, j, k, True).start()

                        @pl.when(k < NY - 1)
                        def _():
                            ag_copy(st, sign, j, k, False).start()

        done = r - (NX - 1)

        @pl.when(done >= 0)
        def _():
            for st, (y_first, sign) in enumerate(streams):
                _, py = where(sign, 0, done)
                acc[st] += jnp.dot(gu_t[py], x_buf[st, py], preferred_element_type=F32)

    for st in range(4):
        gate = acc[st, 0:hidden, :]
        hid[st] = (gate / (1.0 + jnp.exp(-gate)) * acc[st, hidden:2 * hidden, :]).astype(BF)

    def rs_copy(st, sign, j, k, dst, sem, along_x):
        return pltpu.make_async_remote_copy(
            src_ref=piece(o_buf, st, sign, j, k), dst_ref=dst, send_sem=rs_send.at[st], recv_sem=sem,
            device_id=at_xy(x - sign, y) if along_x else at_xy(x, y - sign), device_id_type=MESH)

    def add_from(st, sign, j, k, ref, sem):
        pltpu.make_async_copy(ref, ref, sem).wait()
        own = piece(o_buf, st, sign, j, k)
        own[...] = (own[...].astype(F32) + ref[...].astype(F32)).astype(BF)

    @pl.loop(0, NX + NY - 1)
    def _(r):
        fresh = NY - 1 - r

        @pl.when(fresh >= 0)
        def _():
            for st, (y_first, sign) in enumerate(streams):
                _, py = where(sign, 0, fresh)
                o_buf[st, py] = jnp.dot(down_t[py], hid[st], preferred_element_type=F32).astype(BF)

        for j in range(NX - 1, -1, -1):
            k = NX + NY - 2 - r - j

            @pl.when((k >= 0) & (k < NY))
            def _():
                for st, (y_first, sign) in enumerate(streams):
                    main = piece(r_main, st, sign, j, k)
                    if y_first:
                        if j < NX - 1:
                            add_from(st, sign, j, k, main, rs_recv.at[st, j, k])
                        if j > 0:
                            rs_copy(st, sign, j, k, main, rs_recv.at[st, j - 1, k], True).start()
                        else:
                            @pl.when(k < NY - 1)
                            def _():
                                add_from(st, sign, j, k, r_turn.at[st, k], turn_recv.at[st, k])

                            @pl.when(k > 0)
                            def _():
                                rs_copy(st, sign, j, k, r_turn.at[st, k - 1], turn_recv.at[st, k - 1], False).start()
                    else:
                        @pl.when(k < NY - 1)
                        def _():
                            add_from(st, sign, j, k, main, rs_recv.at[st, j, k])

                        @pl.when(k > 0)
                        def _():
                            rs_copy(st, sign, j, k, main, rs_recv.at[st, j, k - 1], False).start()

                        @pl.when(k == 0)
                        def _():
                            if j < NX - 1:
                                add_from(st, sign, j, k, r_turn.at[st, j], turn_recv.at[st, j])
                            if j > 0:
                                rs_copy(st, sign, j, k, r_turn.at[st, j - 1], turn_recv.at[st, j - 1], True).start()

    def ret_copy(dest, src):
        return pltpu.make_async_remote_copy(
            src_ref=ret_out.at[dest], dst_ref=ret_in.at[src], send_sem=ret_send, recv_sem=ret_recv.at[src],
            device_id=(dp, dest), device_id_type=MESH)

    for st, (y_first, sign) in enumerate(streams):
        total = piece(o_buf, st, sign, 0, 0)[...]
        spread = lax.dot_general(
            total, sel[...], (((1,), (1,)), ((), ())), preferred_element_type=F32).astype(BF)
        for i in range(group):
            ret_out[st * group + i] = spread[:, i * LANES:(i + 1) * LANES]
    ret_in[me] = ret_out[me]
    for p in range(1, n_exp):
        ret_copy(lax.rem(me + p, n_exp), me).start()

    weight = scores_ref[...].astype(F32)
    weight = weight / (weight[:, 0:1] + weight[:, 1:2])
    part0 = jnp.zeros((rows, width), F32)
    part1 = jnp.zeros((rows, width), F32)
    for s in range(n_exp):
        @pl.when(s != me)
        def _():
            pltpu.make_async_copy(ret_in.at[s], ret_in.at[s], ret_recv.at[s]).wait()
        got = ret_in[s]
        dims = (((1,), (1,)), ((), ()))
        cols = slice(s * LANES, (s + 1) * LANES)
        part0 += lax.dot_general(pick0[:, cols], got, dims, preferred_element_type=F32)
        part1 += lax.dot_general(pick1[:, cols], got, dims, preferred_element_type=F32)
    out_ref[...] = (part0 * weight[:, 0:1] + part1 * weight[:, 1:2]).astype(BF)

    sent = pl.ds(0, n_exp - 1)
    pltpu.make_async_copy(disp_out.at[sent], disp_out.at[sent], disp_send).wait()
    pltpu.make_async_copy(ret_out.at[sent], ret_out.at[sent], ret_send).wait()
    for st in range(4):
        for buf, sem in ((x_buf, ag_send), (o_buf, rs_send)):
            most = buf.at[st, pl.ds(0, NY - 1)]
            rest = buf.at[st, NY - 1, pl.ds(0, (NX - 1) * width)]
            pltpu.make_async_copy(most, most, sem.at[st]).wait()
            pltpu.make_async_copy(rest, rest, sem.at[st]).wait()


def shards(tokens, routes, scores, gate_weight, up_weight, down_weight):
    n_exp = lax.axis_size("expert")
    rows, width = tokens.shape
    _, feats, hidden = gate_weight.shape
    cap = 3 * rows // n_exp
    group = n_exp // 4
    span = group * cap
    split = (NX, NY, width, hidden)
    dma = pltpu.SemaphoreType.DMA
    vmem = pl.BlockSpec(memory_space=pltpu.VMEM)
    hbm = pl.BlockSpec(memory_space=pl.ANY)
    return pl.pallas_call(
        moe_kernel,
        out_shape=jax.ShapeDtypeStruct((rows, width), BF),
        in_specs=[vmem, vmem, vmem, hbm, hbm, hbm],
        out_specs=vmem,
        scratch_shapes=[
            pltpu.VMEM(split, BF),
            pltpu.VMEM(split, BF),
            pltpu.VMEM((hidden, feats), BF),
            pltpu.VMEM((NY, 2 * hidden, NX * width), BF),
            pltpu.VMEM((NY, NX * width, hidden), BF),
            pltpu.VMEM((group * LANES, span), BF),
            pltpu.VMEM((n_exp, width, LANES), BF),
            pltpu.VMEM((n_exp, width, LANES), BF),
            pltpu.VMEM((4, NY, NX * width, span), BF),
            pltpu.VMEM((4, 2 * hidden, span), F32),
            pltpu.VMEM((4, hidden, span), BF),
            pltpu.VMEM((4, NY, NX * width, span), BF),
            pltpu.VMEM((4, NY, NX * width, span), BF),
            pltpu.VMEM((4, NY, width, span), BF),
            pltpu.VMEM((n_exp, width, LANES), BF),
            pltpu.VMEM((n_exp, width, LANES), BF),
            pltpu.VMEM((rows, n_exp * LANES), BF),
            pltpu.VMEM((rows, n_exp * LANES), BF),
            dma((3,)), dma, dma((n_exp,)),
            dma((4,)), dma((4, NX, NY)),
            dma((4,)), dma((4, NX, NY)), dma((4, NY)),
            dma, dma((n_exp,)),
        ],
        compiler_params=pltpu.CompilerParams(
            collective_id=0, has_side_effects=True, vmem_limit_bytes=60 * 1024 * 1024),
    )(
        tokens, routes, scores,
        gate_weight[0].reshape(split), up_weight[0].reshape(split), down_weight[0],
    )


def solution(mesh):
    return jax.shard_map(
        shards,
        mesh=mesh,
        in_specs=(
            P("expert", "dp"),
            P("expert", None),
            P("expert", None),
            P("expert", None, "dp"),
            P("expert", None, "dp"),
            P("expert", "dp", None),
        ),
        out_specs=P("expert", "dp"),
        check_vma=False,
    )
```

```python
import functools

import jax
import jax.numpy as jnp
from jax import lax
from jax.experimental import pallas as pl
from jax.experimental.pallas import tpu as pltpu
from jax.sharding import PartitionSpec as P

MESH = pl.DeviceIdType.MESH
NX, NY = 4, 8
LANES = 128
BF, F32 = jnp.bfloat16, jnp.float32


def moe_kernel(
    tokens_ref, routes_ref, scores_ref, gate_hbm, up_hbm, down_hbm, out_ref,
    gate_raw, up_raw, down_raw, gu_t, down_t, sel, disp_out, disp_in,
    x_buf, acc, hid, o_buf, r_main, r_turn, ret_out, ret_in, pick0, pick1,
    load_sem, disp_send, disp_recv, ag_send, ag_recv, rs_send, rs_recv, turn_recv, ret_send, ret_recv,
):
    n_exp = disp_in.shape[0]
    width, rows = tokens_ref.shape
    group = n_exp // 4
    span = x_buf.shape[3]
    cap = span // group
    hidden = gate_raw.shape[3]
    dp = lax.axis_index("dp")
    me = lax.axis_index("expert")
    x, y = dp // NY, dp % NY

    def at_xy(px, py):
        return (lax.rem(px + NX, NX) * NY + lax.rem(py + NY, NY), me)

    loads = [
        pltpu.make_async_copy(src, dst, load_sem.at[i])
        for i, (src, dst) in enumerate(((gate_hbm, gate_raw), (up_hbm, up_raw), (down_hbm, down_raw)))
    ]
    for load in loads:
        load.start()

    barrier = pltpu.get_barrier_semaphore()
    for target in (at_xy(x + 1, y), at_xy(x - 1, y), at_xy(x, y + 1), at_xy(x, y - 1)):
        pl.semaphore_signal(barrier, inc=1, device_id=target, device_id_type=MESH)
    for p in range(1, n_exp):
        pl.semaphore_signal(barrier, inc=1, device_id=(dp, lax.rem(me + p, n_exp)), device_id_type=MESH)

    first, second = routes_ref[0:1, :], routes_ref[1:2, :]
    expert_at = lax.broadcasted_iota(jnp.int32, (n_exp, rows), 0)
    is_first = (expert_at == first).astype(F32)
    is_second = (expert_at == second).astype(F32)
    earlier_mask = (
        lax.broadcasted_iota(jnp.int32, (rows, rows), 0) < lax.broadcasted_iota(jnp.int32, (rows, rows), 1)
    ).astype(F32).astype(BF)
    earlier = jnp.dot((is_first + is_second).astype(BF), earlier_mask, preferred_element_type=F32)
    slot0 = first * LANES + jnp.sum(is_first * earlier, axis=0, keepdims=True).astype(jnp.int32)
    slot1 = second * LANES + jnp.sum(is_second * earlier, axis=0, keepdims=True).astype(jnp.int32)

    tok = tokens_ref[...]
    wide = group * LANES
    slot_at = lax.broadcasted_iota(jnp.int32, (wide, rows), 0)
    last_dims = (((1,), (1,)), ((), ()))
    for q in range(4):
        ids = slot_at + q * wide
        picked = ((ids == slot0) | (ids == slot1)).astype(F32).astype(BF)
        packed = lax.dot_general(tok, picked, last_dims, preferred_element_type=F32).astype(BF)
        for i in range(group):
            disp_out[q * group + i] = packed[:, i * LANES:(i + 1) * LANES]
    disp_in[me] = disp_out[me]

    pl.semaphore_wait(barrier, 4 + n_exp - 1)

    def disp_copy(dest, src):
        return pltpu.make_async_remote_copy(
            src_ref=disp_out.at[dest], dst_ref=disp_in.at[src], send_sem=disp_send, recv_sem=disp_recv.at[src],
            device_id=(dp, dest), device_id_type=MESH)

    for p in range(1, n_exp):
        disp_copy(lax.rem(me + p, n_exp), me).start()

    si = lax.broadcasted_iota(jnp.int32, (wide, span), 0)
    sl = lax.broadcasted_iota(jnp.int32, (wide, span), 1)
    rank_in = si % LANES
    sel[...] = ((sl == (si // LANES) * cap + rank_in) & (rank_in < cap)).astype(F32).astype(BF)

    for st in range(4):
        acc[st] = jnp.zeros(acc.shape[1:], F32)

    for q in range(4):
        ids = slot_at + q * wide
        pick0[q * wide:(q + 1) * wide, :] = (ids == slot0).astype(F32).astype(BF)
        pick1[q * wide:(q + 1) * wide, :] = (ids == slot1).astype(F32).astype(BF)

    def turn_gate_up(yy):
        g = gate_raw[:, yy].reshape(NX * width, hidden)
        u = up_raw[:, yy].reshape(NX * width, hidden)
        gu_t[yy, 0:hidden, :] = g.T
        gu_t[yy, hidden:2 * hidden, :] = u.T

    def turn_down(c):
        turned = down_raw[:, pl.ds(pl.multiple_of(c * LANES, LANES), LANES)].T
        for h in range(LANES // width):
            block = c * (LANES // width) + h
            xx, yy = block // NY, block % NY
            down_t[yy, pl.ds(pl.multiple_of(xx * width, width), width), :] = turned[h * width:(h + 1) * width, :]

    streams = [(True, 1), (True, -1), (False, 1), (False, -1)]

    def where(sign, j, k):
        px = lax.rem(x - sign * j + 2 * NX, NX)
        py = lax.rem(y - sign * k + 2 * NY, NY)
        return px, py

    def piece(buf, st, sign, j, k):
        px, py = where(sign, j, k)
        return buf.at[st, py, pl.ds(pl.multiple_of(px * width, width), width)]

    def ag_copy(st, sign, j, k, along_x):
        ref = piece(x_buf, st, sign, j, k)
        return pltpu.make_async_remote_copy(
            src_ref=ref, dst_ref=ref, send_sem=ag_send.at[st],
            recv_sem=ag_recv.at[st, j + 1, k] if along_x else ag_recv.at[st, j, k + 1],
            device_id=at_xy(x + sign, y) if along_x else at_xy(x, y + sign), device_id_type=MESH)

    def ag_wait(st, sign, j, k):
        ref = piece(x_buf, st, sign, j, k)
        pltpu.make_async_copy(ref, ref, ag_recv.at[st, j, k]).wait()

    for st, (y_first, sign) in enumerate(streams):
        for s in range(st * group, (st + 1) * group):
            @pl.when(s != me)
            def _():
                pltpu.make_async_copy(disp_in.at[s], disp_in.at[s], disp_recv.at[s]).wait()
        packed = jnp.concatenate([disp_in[st * group + i] for i in range(group)], axis=1)
        x_buf[st, y, pl.ds(pl.multiple_of(x * width, width), width), :] = jnp.dot(
            packed, sel[...], preferred_element_type=F32).astype(BF)
        ag_copy(st, sign, 0, 0, True).start()
        ag_copy(st, sign, 0, 0, False).start()

    for load in loads:
        load.wait()

    @pl.loop(0, NY // 2)
    def _(yy):
        turn_gate_up(yy)

    @pl.loop(1, NX + NY - 1)
    def _(r):
        for j in range(NX):
            k = r - j

            @pl.when((k >= 0) & (k < NY))
            def _():
                for st, (y_first, sign) in enumerate(streams):
                    ag_wait(st, sign, j, k)
                    if y_first:
                        if j < NX - 1:
                            ag_copy(st, sign, j, k, True).start()
                        if j == 0:
                            @pl.when(k < NY - 1)
                            def _():
                                ag_copy(st, sign, j, k, False).start()
                    else:
                        if j < NX - 1:
                            @pl.when(k == 0)
                            def _():
                                ag_copy(st, sign, j, k, True).start()

                        @pl.when(k < NY - 1)
                        def _():
                            ag_copy(st, sign, j, k, False).start()

        @pl.when(r < NX - 1)
        def _():
            for h in range(2):
                turn_gate_up(NY // 2 + 2 * (r - 1) + h)

        done = r - (NX - 1)

        @pl.when(done >= 0)
        def _():
            for st, (y_first, sign) in enumerate(streams):
                _, py = where(sign, 0, done)
                acc[st] += jnp.dot(gu_t[py], x_buf[st, py], preferred_element_type=F32)
            for h in range(2):
                turn_down(2 * done + h)

    for st in range(4):
        gate = acc[st, 0:hidden, :]
        hid[st] = (gate / (1.0 + jnp.exp(-gate)) * acc[st, hidden:2 * hidden, :]).astype(BF)

    def rs_copy(st, sign, j, k, dst, sem, along_x):
        return pltpu.make_async_remote_copy(
            src_ref=piece(o_buf, st, sign, j, k), dst_ref=dst, send_sem=rs_send.at[st], recv_sem=sem,
            device_id=at_xy(x - sign, y) if along_x else at_xy(x, y - sign), device_id_type=MESH)

    def add_from(st, sign, j, k, ref, sem):
        pltpu.make_async_copy(ref, ref, sem).wait()
        own = piece(o_buf, st, sign, j, k)
        own[...] = (own[...].astype(F32) + ref[...].astype(F32)).astype(BF)

    @pl.loop(0, NX + NY - 1)
    def _(r):
        fresh = NY - 1 - r

        @pl.when(fresh >= 0)
        def _():
            for st, (y_first, sign) in enumerate(streams):
                _, py = where(sign, 0, fresh)
                o_buf[st, py] = jnp.dot(down_t[py], hid[st], preferred_element_type=F32).astype(BF)

        for j in range(NX - 1, -1, -1):
            k = NX + NY - 2 - r - j

            @pl.when((k >= 0) & (k < NY))
            def _():
                for st, (y_first, sign) in enumerate(streams):
                    main = piece(r_main, st, sign, j, k)
                    if y_first:
                        if j < NX - 1:
                            add_from(st, sign, j, k, main, rs_recv.at[st, j, k])
                        if j > 0:
                            rs_copy(st, sign, j, k, main, rs_recv.at[st, j - 1, k], True).start()
                        else:
                            @pl.when(k < NY - 1)
                            def _():
                                add_from(st, sign, j, k, r_turn.at[st, k], turn_recv.at[st, k])

                            @pl.when(k > 0)
                            def _():
                                rs_copy(st, sign, j, k, r_turn.at[st, k - 1], turn_recv.at[st, k - 1], False).start()
                    else:
                        @pl.when(k < NY - 1)
                        def _():
                            add_from(st, sign, j, k, main, rs_recv.at[st, j, k])

                        @pl.when(k > 0)
                        def _():
                            rs_copy(st, sign, j, k, main, rs_recv.at[st, j, k - 1], False).start()

                        @pl.when(k == 0)
                        def _():
                            if j < NX - 1:
                                add_from(st, sign, j, k, r_turn.at[st, j], turn_recv.at[st, j])
                            if j > 0:
                                rs_copy(st, sign, j, k, r_turn.at[st, j - 1], turn_recv.at[st, j - 1], True).start()

    def ret_copy(dest, src):
        return pltpu.make_async_remote_copy(
            src_ref=ret_out.at[dest], dst_ref=ret_in.at[src], send_sem=ret_send, recv_sem=ret_recv.at[src],
            device_id=(dp, dest), device_id_type=MESH)

    for st, (y_first, sign) in enumerate(streams):
        total = piece(o_buf, st, sign, 0, 0)[...]
        spread = lax.dot_general(total, sel[...], last_dims, preferred_element_type=F32).astype(BF)
        for i in range(group):
            dest = st * group + i
            ret_out[dest] = spread[:, i * LANES:(i + 1) * LANES]

            @pl.when(dest != me)
            def _():
                ret_copy(dest, me).start()
    ret_in[me] = ret_out[me]

    weight = scores_ref[...].astype(F32)
    weight = weight / (weight[0:1, :] + weight[1:2, :])
    part0 = jnp.zeros((width, rows), F32)
    part1 = jnp.zeros((width, rows), F32)
    for q in range(4):
        for s in range(q * group, (q + 1) * group):
            @pl.when(s != me)
            def _():
                pltpu.make_async_copy(ret_in.at[s], ret_in.at[s], ret_recv.at[s]).wait()
        got = jnp.concatenate([ret_in[q * group + i] for i in range(group)], axis=1)
        cut = slice(q * wide, (q + 1) * wide)
        part0 += jnp.dot(got, pick0[cut, :], preferred_element_type=F32)
        part1 += jnp.dot(got, pick1[cut, :], preferred_element_type=F32)
    out_ref[...] = (part0 * weight[0:1, :] + part1 * weight[1:2, :]).astype(BF)

    sent = pl.ds(0, n_exp - 1)
    pltpu.make_async_copy(disp_out.at[sent], disp_out.at[sent], disp_send).wait()
    pltpu.make_async_copy(ret_out.at[sent], ret_out.at[sent], ret_send).wait()
    for st in range(4):
        for buf, sem in ((x_buf, ag_send), (o_buf, rs_send)):
            most = buf.at[st, pl.ds(0, NY - 1)]
            rest = buf.at[st, NY - 1, pl.ds(0, (NX - 1) * width)]
            pltpu.make_async_copy(most, most, sem.at[st]).wait()
            pltpu.make_async_copy(rest, rest, sem.at[st]).wait()


def shards(tokens, routes, scores, gate_weight, up_weight, down_weight):
    n_exp = lax.axis_size("expert")
    rows, width = tokens.shape
    _, feats, hidden = gate_weight.shape
    cap = 3 * rows // n_exp
    group = n_exp // 4
    span = group * cap
    split = (NX, NY, width, hidden)
    dma = pltpu.SemaphoreType.DMA
    vmem = pl.BlockSpec(memory_space=pltpu.VMEM)
    hbm = pl.BlockSpec(memory_space=pl.ANY)
    return pl.pallas_call(
        moe_kernel,
        out_shape=jax.ShapeDtypeStruct((width, rows), BF),
        in_specs=[vmem, vmem, vmem, hbm, hbm, hbm],
        out_specs=vmem,
        scratch_shapes=[
            pltpu.VMEM(split, BF),
            pltpu.VMEM(split, BF),
            pltpu.VMEM((hidden, feats), BF),
            pltpu.VMEM((NY, 2 * hidden, NX * width), BF),
            pltpu.VMEM((NY, NX * width, hidden), BF),
            pltpu.VMEM((group * LANES, span), BF),
            pltpu.VMEM((n_exp, width, LANES), BF),
            pltpu.VMEM((n_exp, width, LANES), BF),
            pltpu.VMEM((4, NY, NX * width, span), BF),
            pltpu.VMEM((4, 2 * hidden, span), F32),
            pltpu.VMEM((4, hidden, span), BF),
            pltpu.VMEM((4, NY, NX * width, span), BF),
            pltpu.VMEM((4, NY, NX * width, span), BF),
            pltpu.VMEM((4, NY, width, span), BF),
            pltpu.VMEM((n_exp, width, LANES), BF),
            pltpu.VMEM((n_exp, width, LANES), BF),
            pltpu.VMEM((n_exp * LANES, rows), BF),
            pltpu.VMEM((n_exp * LANES, rows), BF),
            dma((3,)), dma, dma((n_exp,)),
            dma((4,)), dma((4, NX, NY)),
            dma((4,)), dma((4, NX, NY)), dma((4, NY)),
            dma, dma((n_exp,)),
        ],
        compiler_params=pltpu.CompilerParams(
            collective_id=0, has_side_effects=True, vmem_limit_bytes=60 * 1024 * 1024),
    )(
        tokens.T, routes.T, scores.T,
        gate_weight[0].reshape(split), up_weight[0].reshape(split), down_weight[0],
    ).T


def solution(mesh):
    return jax.shard_map(
        shards,
        mesh=mesh,
        in_specs=(
            P("expert", "dp"),
            P("expert", None),
            P("expert", None),
            P("expert", None, "dp"),
            P("expert", None, "dp"),
            P("expert", "dp", None),
        ),
        out_specs=P("expert", "dp"),
        check_vma=False,
    )
```

```python
import functools

import jax
import jax.numpy as jnp
from jax import lax
from jax.experimental import pallas as pl
from jax.experimental.pallas import tpu as pltpu
from jax.sharding import PartitionSpec as P

MESH = pl.DeviceIdType.MESH
NX, NY = 4, 8
LANES = 128
BF, F32 = jnp.bfloat16, jnp.float32


OUT_ORDER = (0, 1, 3, 2)
BACK_ORDER = (2, 1, 3, 0)


def moe_kernel(
    tokens_ref, routes_ref, scores_ref, gate_hbm, up_hbm, down_hbm, out_ref,
    gate_w, up_w, down_w, down_t, sel, disp_out, disp_in,
    x_side, x_buf, acc, hid, o_buf, r_main, r_turn, ret_out, ret_in, pick0, pick1,
    load_sem, w_send, w_recv, down_recv, disp_send, disp_recv, side_send, ag_send, ag_recv,
    rs_send, rs_recv, turn_recv, ret_send, ret_recv,
):
    n_exp = disp_in.shape[0]
    width, rows = tokens_ref.shape
    group = n_exp // 4
    span = x_buf.shape[3]
    cap = span // group
    hidden = gate_hbm.shape[3]
    half = hidden // 2
    feats = NX * width
    dp = lax.axis_index("dp")
    me = lax.axis_index("expert")
    x, y = dp // NY, dp % NY
    parity = x % 2
    signs = (1, -1)

    def at_xy(px, py):
        return (lax.rem(px + NX, NX) * NY + lax.rem(py + NY, NY), me)

    own_cols = pl.ds(0, hidden)
    loads = [
        pltpu.make_async_copy(gate_hbm, gate_w.at[:, :, :, own_cols], load_sem.at[0]),
        pltpu.make_async_copy(up_hbm, up_w.at[:, :, :, own_cols], load_sem.at[1]),
        pltpu.make_async_copy(down_hbm, down_w.at[own_cols], load_sem.at[2]),
    ]
    for load in loads:
        load.start()

    barrier = pltpu.get_barrier_semaphore()
    for target in (at_xy(x + 1, y), at_xy(x - 1, y), at_xy(x + 2, y), at_xy(x, y + 1), at_xy(x, y - 1)):
        pl.semaphore_signal(barrier, inc=1, device_id=target, device_id_type=MESH)
    for p in range(1, n_exp):
        pl.semaphore_signal(barrier, inc=1, device_id=(dp, lax.rem(me + p, n_exp)), device_id_type=MESH)

    first, second = routes_ref[0:1, :], routes_ref[1:2, :]
    expert_at = lax.broadcasted_iota(jnp.int32, (n_exp, rows), 0)
    is_first = (expert_at == first).astype(F32)
    is_second = (expert_at == second).astype(F32)
    earlier_mask = (
        lax.broadcasted_iota(jnp.int32, (rows, rows), 0) < lax.broadcasted_iota(jnp.int32, (rows, rows), 1)
    ).astype(F32).astype(BF)
    earlier = jnp.dot((is_first + is_second).astype(BF), earlier_mask, preferred_element_type=F32)
    slot0 = first * LANES + jnp.sum(is_first * earlier, axis=0, keepdims=True).astype(jnp.int32)
    slot1 = second * LANES + jnp.sum(is_second * earlier, axis=0, keepdims=True).astype(jnp.int32)

    tok = tokens_ref[...]
    wide = group * LANES
    slot_at = lax.broadcasted_iota(jnp.int32, (wide, rows), 0)
    last_dims = (((1,), (1,)), ((), ()))
    for q in range(4):
        ids = slot_at + q * wide
        picked = ((ids == slot0) | (ids == slot1)).astype(F32).astype(BF)
        packed = lax.dot_general(tok, picked, last_dims, preferred_element_type=F32).astype(BF)
        for i in range(group):
            disp_out[q * group + i] = packed[:, i * LANES:(i + 1) * LANES]
    disp_in[me] = disp_out[me]

    pl.semaphore_wait(barrier, 5 + n_exp - 1)

    def disp_copy(dest, src):
        return pltpu.make_async_remote_copy(
            src_ref=disp_out.at[dest], dst_ref=disp_in.at[src], send_sem=disp_send, recv_sem=disp_recv.at[src],
            device_id=(dp, dest), device_id_type=MESH)

    for p in range(1, n_exp):
        disp_copy(lax.rem(me + p, n_exp), me).start()

    def sides():
        return ((0, 1, half, hidden), (1, -1, 0, hidden + half))

    def send_gate_up(back):
        yy = lax.rem(y + back + NY, NY)
        for side, step, src, dst in sides():
            for mat, (hbm, buf) in enumerate(((gate_hbm, gate_w), (up_hbm, up_w))):
                pltpu.make_async_remote_copy(
                    src_ref=hbm.at[:, yy, :, pl.ds(src, half)], dst_ref=buf.at[:, yy, :, pl.ds(dst, half)],
                    send_sem=w_send.at[mat], recv_sem=w_recv.at[mat, side, yy],
                    device_id=at_xy(x + step, y), device_id_type=MESH).start()

    def wait_gate_up(back):
        yy = lax.rem(y + back + NY, NY)
        for side, step, src, dst in sides():
            for mat, buf in enumerate((gate_w, up_w)):
                ref = buf.at[:, yy, :, pl.ds(dst, half)]
                pltpu.make_async_copy(ref, ref, w_recv.at[mat, side, yy]).wait()

    def send_down():
        for side, step, src, dst in sides():
            pltpu.make_async_remote_copy(
                src_ref=down_hbm.at[pl.ds(src, half)], dst_ref=down_w.at[pl.ds(dst, half)],
                send_sem=w_send.at[2], recv_sem=down_recv.at[side],
                device_id=at_xy(x + step, y), device_id_type=MESH).start()

    send_gate_up(0)
    send_gate_up(1)
    send_gate_up(-1)

    si = lax.broadcasted_iota(jnp.int32, (wide, span), 0)
    sl = lax.broadcasted_iota(jnp.int32, (wide, span), 1)
    rank_in = si % LANES
    sel[...] = ((sl == (si // LANES) * cap + rank_in) & (rank_in < cap)).astype(F32).astype(BF)

    for st in range(2):
        for mat in range(2):
            acc[st, mat] = jnp.zeros(acc.shape[2:], F32)

    for q in range(4):
        ids = slot_at + q * wide
        pick0[q * wide:(q + 1) * wide, :] = (ids == slot0).astype(F32).astype(BF)
        pick1[q * wide:(q + 1) * wide, :] = (ids == slot1).astype(F32).astype(BF)

    def piece(buf, st, i, k):
        px = lax.rem(x + i, NX)
        py = lax.rem(y - signs[st] * k + 2 * NY, NY)
        return buf.at[st, py, pl.ds(pl.multiple_of(px * width, width), width)]

    def arrive(quarter):
        for i in range(group):
            s = quarter * group + i

            @pl.when(s != me)
            def _():
                pltpu.make_async_copy(disp_in.at[s], disp_in.at[s], disp_recv.at[s]).wait()
        packed = jnp.concatenate([disp_in[quarter * group + i] for i in range(group)], axis=1)
        return jnp.dot(packed, sel[...], preferred_element_type=F32).astype(BF)

    def ag_wait(st, i, k):
        ref = piece(x_buf, st, i, k)
        pltpu.make_async_copy(ref, ref, ag_recv.at[st, k, i]).wait()

    def ag_forward(st, i, k):
        ref = piece(x_buf, st, i, k)
        pltpu.make_async_remote_copy(
            src_ref=ref, dst_ref=ref, send_sem=ag_send.at[st], recv_sem=ag_recv.at[st, k + 1, i],
            device_id=at_xy(x, y + signs[st]), device_id_type=MESH).start()

    def side_copy(src, st, step):
        return pltpu.make_async_remote_copy(
            src_ref=src, dst_ref=piece(x_buf, st, 0, 0), send_sem=side_send.at[st],
            recv_sem=ag_recv.at[st, 0, (NX - step) % NX],
            device_id=at_xy(x + step, y), device_id_type=MESH)

    for st in range(2):
        own = piece(x_buf, st, 0, 0)
        own[...] = arrive(2 * parity + st)
        side_copy(own, st, 2).start()
        ag_forward(st, 0, 0)
    for st in range(2):
        x_side[st] = arrive(2 * (1 - parity) + st)
        side_copy(x_side.at[st], st, 1).start()
        side_copy(x_side.at[st], st, 3).start()
    for load in loads:
        load.wait()
    for i in OUT_ORDER[1:]:
        for st in range(2):
            ag_wait(st, i, 0)
            ag_forward(st, i, 0)
    send_gate_up(2)
    send_gate_up(-2)

    def grow(st, mat, k):
        py = lax.rem(y - signs[st] * k + 2 * NY, NY)
        weights = (gate_w, up_w)[mat][:, py].reshape(feats, 2 * hidden)
        acc[st, mat] += lax.dot_general(
            x_buf[st, py], weights, (((0,), (0,)), ((), ())), preferred_element_type=F32)

    def turn_down(c, rows_from):
        turned = down_w[rows_from:rows_from + hidden, pl.ds(pl.multiple_of(c * LANES, LANES), LANES)].T
        for h in range(LANES // width):
            block = c * (LANES // width) + h
            xx, yy = block // NY, block % NY
            down_t[yy, pl.ds(pl.multiple_of(xx * width, width), width), rows_from:rows_from + hidden] = (
                turned[h * width:(h + 1) * width, :])

    col_blocks = NX * NY * width // LANES

    @pl.loop(1, NY)
    def _(k):
        @pl.when(k == NY - 1)
        def _():
            for side, step, src, dst in sides():
                ref = down_w.at[pl.ds(dst, half)]
                pltpu.make_async_copy(ref, ref, down_recv.at[side]).wait()

            @pl.loop(0, col_blocks)
            def _(c):
                turn_down(c, hidden)

        for n, i in enumerate(OUT_ORDER):
            for st in range(2):
                ag_wait(st, i, k)

                @pl.when(k < NY - 1)
                def _():
                    ag_forward(st, i, k)

            if n == 0:
                @pl.when(k - 1 <= NY // 2)
                def _():
                    wait_gate_up(1 - k)
            if n == 2:
                @pl.when((k - 1 >= 1) & (k - 1 < NY // 2))
                def _():
                    wait_gate_up(k - 1)
            grow(n // 2, n % 2, k - 1)

        @pl.when(k == 1)
        def _():
            send_gate_up(3)
            send_gate_up(-3)

        @pl.when(k == 2)
        def _():
            send_gate_up(4)
            send_down()

        @pl.when(k <= 4)
        def _():
            for h in range(col_blocks // 4):
                turn_down((k - 1) * (col_blocks // 4) + h, 0)

    def produce(st, k):
        py = lax.rem(y - signs[st] * k + 2 * NY, NY)
        o_buf[st, py] = lax.dot_general(
            down_t[py], hid[st], last_dims, preferred_element_type=F32).astype(BF)

    def rs_forward(st, i, k):
        pltpu.make_async_remote_copy(
            src_ref=piece(o_buf, st, i, k), dst_ref=piece(r_main, st, i, k), send_sem=rs_send.at[st],
            recv_sem=rs_recv.at[st, k - 1, i], device_id=at_xy(x, y - signs[st]), device_id_type=MESH).start()

    def rs_add(st, i, k):
        got = piece(r_main, st, i, k)
        pltpu.make_async_copy(got, got, rs_recv.at[st, k, i]).wait()
        own = piece(o_buf, st, i, k)
        own[...] = (own[...].astype(F32) + got[...].astype(F32)).astype(BF)

    for st in range(2):
        for mat in range(2):
            grow(st, mat, NY - 1)
        gate = acc[st, 0]
        hid[st] = (gate / (1.0 + jnp.exp(-gate)) * acc[st, 1]).astype(BF)
        produce(st, NY - 1)
        for i in BACK_ORDER:
            rs_forward(st, i, NY - 1)
    for st in range(2):
        produce(st, NY - 2)

    @pl.loop(1, NY - 1)
    def _(r):
        k = NY - 1 - r
        for n, i in enumerate(BACK_ORDER):
            for st in range(2):
                rs_add(st, i, k)
                rs_forward(st, i, k)
            if n < 2:
                produce(n, k - 1)

    for i in BACK_ORDER:
        for st in range(2):
            rs_add(st, i, 0)
            if i > 0:
                pltpu.make_async_remote_copy(
                    src_ref=piece(o_buf, st, i, 0), dst_ref=r_turn.at[st, i - 1], send_sem=rs_send.at[st],
                    recv_sem=turn_recv.at[st, i - 1], device_id=at_xy(x + i, y), device_id_type=MESH).start()

    def ret_copy(dest, src):
        return pltpu.make_async_remote_copy(
            src_ref=ret_out.at[dest], dst_ref=ret_in.at[src], send_sem=ret_send, recv_sem=ret_recv.at[src],
            device_id=(dp, dest), device_id_type=MESH)

    def turn_wait(st, i):
        ref = r_turn.at[st, i - 1]
        pltpu.make_async_copy(ref, ref, turn_recv.at[st, i - 1]).wait()
        return r_turn[st, i - 1].astype(F32)

    def give_back(quarter, total):
        spread = lax.dot_general(total.astype(BF), sel[...], last_dims, preferred_element_type=F32).astype(BF)
        for i in range(group):
            dest = quarter * group + i
            ret_out[dest] = spread[:, i * LANES:(i + 1) * LANES]

            @pl.when(dest != me)
            def _():
                ret_copy(dest, me).start()

    for st in range(2):
        give_back(2 * parity + st, piece(o_buf, st, 0, 0)[...].astype(F32) + turn_wait(st, 2))
    for st in range(2):
        give_back(2 * (1 - parity) + st, turn_wait(st, 1) + turn_wait(st, 3))
    ret_in[me] = ret_out[me]

    weight = scores_ref[...].astype(F32)
    weight = weight / (weight[0:1, :] + weight[1:2, :])
    part0 = jnp.zeros((width, rows), F32)
    part1 = jnp.zeros((width, rows), F32)
    for q in range(4):
        for s in range(q * group, (q + 1) * group):
            @pl.when(s != me)
            def _():
                pltpu.make_async_copy(ret_in.at[s], ret_in.at[s], ret_recv.at[s]).wait()
        got = jnp.concatenate([ret_in[q * group + i] for i in range(group)], axis=1)
        cut = slice(q * wide, (q + 1) * wide)
        part0 += jnp.dot(got, pick0[cut, :], preferred_element_type=F32)
        part1 += jnp.dot(got, pick1[cut, :], preferred_element_type=F32)
    out_ref[...] = (part0 * weight[0:1, :] + part1 * weight[1:2, :]).astype(BF)

    def drained(ref, sem):
        pltpu.make_async_copy(ref, ref, sem).wait()

    sent = pl.ds(0, n_exp - 1)
    drained(disp_out.at[sent], disp_send)
    drained(ret_out.at[sent], ret_send)
    drained(gate_w.at[:, :, :, own_cols], w_send.at[0])
    drained(up_w.at[:, :, :, own_cols], w_send.at[1])
    drained(down_w.at[own_cols], w_send.at[2])
    for st in range(2):
        drained(x_buf.at[st, 0, pl.ds(0, 3 * width)], side_send.at[st])
        drained(x_buf.at[st, pl.ds(0, NY - 1)], ag_send.at[st])
        drained(o_buf.at[st, pl.ds(0, NY - 1)], rs_send.at[st])
        drained(o_buf.at[st, 0, pl.ds(0, 3 * width)], rs_send.at[st])


def shards(tokens, routes, scores, gate_weight, up_weight, down_weight):
    n_exp = lax.axis_size("expert")
    rows, width = tokens.shape
    _, feats, hidden = gate_weight.shape
    cap = 3 * rows // n_exp
    group = n_exp // 4
    span = group * cap
    split = (NX, NY, width, hidden)
    both = (NX, NY, width, 2 * hidden)
    pieces = (2, NY, NX * width, span)
    dma = pltpu.SemaphoreType.DMA
    vmem = pl.BlockSpec(memory_space=pltpu.VMEM)
    hbm = pl.BlockSpec(memory_space=pl.ANY)
    return pl.pallas_call(
        moe_kernel,
        out_shape=jax.ShapeDtypeStruct((width, rows), BF),
        in_specs=[vmem, vmem, vmem, hbm, hbm, hbm],
        out_specs=vmem,
        scratch_shapes=[
            pltpu.VMEM(both, BF),
            pltpu.VMEM(both, BF),
            pltpu.VMEM((2 * hidden, feats), BF),
            pltpu.VMEM((NY, NX * width, 2 * hidden), BF),
            pltpu.VMEM((group * LANES, span), BF),
            pltpu.VMEM((n_exp, width, LANES), BF),
            pltpu.VMEM((n_exp, width, LANES), BF),
            pltpu.VMEM((2, width, span), BF),
            pltpu.VMEM(pieces, BF),
            pltpu.VMEM((2, 2, span, 2 * hidden), F32),
            pltpu.VMEM((2, span, 2 * hidden), BF),
            pltpu.VMEM(pieces, BF),
            pltpu.VMEM(pieces, BF),
            pltpu.VMEM((2, NX - 1, width, span), BF),
            pltpu.VMEM((n_exp, width, LANES), BF),
            pltpu.VMEM((n_exp, width, LANES), BF),
            pltpu.VMEM((n_exp * LANES, rows), BF),
            pltpu.VMEM((n_exp * LANES, rows), BF),
            dma((3,)), dma((3,)), dma((2, 2, NY)), dma((2,)), dma, dma((n_exp,)),
            dma((2,)), dma((2,)), dma((2, NY, NX)),
            dma((2,)), dma((2, NY, NX)), dma((2, NX - 1)), dma, dma((n_exp,)),
        ],
        compiler_params=pltpu.CompilerParams(
            collective_id=0, has_side_effects=True, vmem_limit_bytes=60 * 1024 * 1024),
    )(
        tokens.T, routes.T, scores.T,
        gate_weight[0].reshape(split), up_weight[0].reshape(split), down_weight[0],
    ).T


def solution(mesh):
    return jax.shard_map(
        shards,
        mesh=mesh,
        in_specs=(
            P("expert", "dp"),
            P("expert", None),
            P("expert", None),
            P("expert", None, "dp"),
            P("expert", None, "dp"),
            P("expert", "dp", None),
        ),
        out_specs=P("expert", "dp"),
        check_vma=False,
    )
```

```python
import functools

import jax
import jax.numpy as jnp
from jax import lax
from jax.experimental import pallas as pl
from jax.experimental.pallas import tpu as pltpu
from jax.sharding import PartitionSpec as P

MESH = pl.DeviceIdType.MESH
NX, NY = 4, 8
LANES = 128
BF, F32 = jnp.bfloat16, jnp.float32


OUT_ORDER = ((0, 3, 1, 2), (0, 1, 3, 2))
BACK_ORDER = (2, 1, 3, 0)


def moe_kernel(
    tokens_ref, routes_ref, scores_ref, gate_hbm, up_hbm, down_hbm, out_ref,
    gate_w, up_w, down_w, down_t, sel, disp_out, disp_in,
    x_side, x_relay, x_buf, acc, hid, o_buf, r_main, r_turn, ret_out, ret_in, pick,
    load_sem, w_send, w_recv, down_recv, disp_send, disp_recv, side_send, relay_recv, ag_send, ag_recv,
    rs_send, rs_recv, turn_recv, ret_send, ret_recv,
):
    n_exp = disp_in.shape[0]
    width, rows = tokens_ref.shape
    group = n_exp // 4
    span = x_buf.shape[3]
    fold = span // group // 2
    hidden = gate_hbm.shape[3]
    half = hidden // 2
    feats = NX * width
    dp = lax.axis_index("dp")
    me = lax.axis_index("expert")
    x, y = dp // NY, dp % NY
    parity = x % 2
    signs = (1, -1)

    def at_xy(px, py):
        return (lax.rem(px + NX, NX) * NY + lax.rem(py + NY, NY), me)

    own_cols = pl.ds(0, hidden)
    loads = [
        pltpu.make_async_copy(hbm.at[:, :, :, pl.ds(h * half, half)], buf.at[h], load_sem.at[2 * mat + h])
        for mat, (hbm, buf) in enumerate(((gate_hbm, gate_w), (up_hbm, up_w)))
        for h in range(2)
    ] + [
        pltpu.make_async_copy(down_hbm, down_w.at[own_cols], load_sem.at[4]),
    ]
    for load in loads:
        load.start()

    barrier = pltpu.get_barrier_semaphore()
    for target in (at_xy(x + 1, y), at_xy(x - 1, y), at_xy(x + 2, y), at_xy(x, y + 1), at_xy(x, y - 1)):
        pl.semaphore_signal(barrier, inc=1, device_id=target, device_id_type=MESH)
    for p in range(1, n_exp):
        pl.semaphore_signal(barrier, inc=1, device_id=(dp, lax.rem(me + p, n_exp)), device_id_type=MESH)

    pl.semaphore_wait(barrier, 5 + n_exp - 1)

    def sides():
        return ((0, 1, half, hidden), (1, -1, 0, hidden + half))

    def send_gate_up(back):
        yy = lax.rem(y + back + NY, NY)
        for side, step, src, dst in sides():
            for mat, buf in enumerate((gate_w, up_w)):
                pltpu.make_async_remote_copy(
                    src_ref=buf.at[src // half, :, yy], dst_ref=buf.at[dst // half, :, yy],
                    send_sem=w_send.at[mat], recv_sem=w_recv.at[mat, side, yy],
                    device_id=at_xy(x + step, y), device_id_type=MESH).start()

    def wait_gate_up(back):
        yy = lax.rem(y + back + NY, NY)
        for side, step, src, dst in sides():
            for mat, buf in enumerate((gate_w, up_w)):
                ref = buf.at[dst // half, :, yy]
                pltpu.make_async_copy(ref, ref, w_recv.at[mat, side, yy]).wait()

    def send_down():
        for side, step, src, dst in sides():
            pltpu.make_async_remote_copy(
                src_ref=down_w.at[pl.ds(src, half)], dst_ref=down_w.at[pl.ds(dst, half)],
                send_sem=w_send.at[2], recv_sem=down_recv.at[side],
                device_id=at_xy(x + step, y), device_id_type=MESH).start()

    for load in loads:
        load.wait()
    send_gate_up(0)
    send_gate_up(1)
    send_gate_up(-1)

    first, second = routes_ref[0:1, :], routes_ref[1:2, :]
    expert_at = lax.broadcasted_iota(jnp.int32, (n_exp, rows), 0)
    is_first = (expert_at == first).astype(F32)
    is_second = (expert_at == second).astype(F32)
    earlier_mask = (
        lax.broadcasted_iota(jnp.int32, (rows, rows), 0) < lax.broadcasted_iota(jnp.int32, (rows, rows), 1)
    ).astype(F32).astype(BF)
    named = is_first + is_second
    earlier = jnp.dot(named.astype(BF), earlier_mask, preferred_element_type=F32)
    rank = jnp.where(named > 0.0, earlier, -1.0)

    tok = tokens_ref[...]
    none = jnp.zeros((width, rows), BF)
    tok_pair = jnp.concatenate(
        [jnp.concatenate([tok, none], axis=1), jnp.concatenate([none, tok], axis=1)], axis=0)
    slot_low = lax.broadcasted_iota(jnp.int32, (fold, rows), 0).astype(F32)
    slot_high = (slot_low + fold).astype(BF)
    slot_low = slot_low.astype(BF)
    last_dims = (((1,), (1,)), ((), ()))
    first_dims = (((0,), (0,)), ((), ()))
    for q in range(4):
        for i in range(group):
            e = q * group + i
            of_slot = jnp.tile(jnp.broadcast_to(rank[e:e + 1, :], (16, rows)).astype(BF), (fold // 16, 1))
            pick[e, :, 0:rows] = jnp.where(slot_low == of_slot, 1.0, 0.0).astype(BF)
            pick[e, :, rows:2 * rows] = jnp.where(slot_high == of_slot, 1.0, 0.0).astype(BF)
        picked = pick[q * group:(q + 1) * group].reshape(group * fold, 2 * rows)
        packed = lax.dot_general(picked, tok_pair, last_dims, preferred_element_type=F32).astype(BF)
        disp_out[q * group:(q + 1) * group] = packed.reshape(group, fold, 2 * width)
    disp_in[me] = disp_out[me]

    def disp_copy(dest, src):
        return pltpu.make_async_remote_copy(
            src_ref=disp_out.at[dest], dst_ref=disp_in.at[src], send_sem=disp_send, recv_sem=disp_recv.at[src],
            device_id=(dp, dest), device_id_type=MESH)

    far_first = sorted(range(1, n_exp), key=lambda p: abs(2 * p - n_exp))
    for p in far_first:
        disp_copy(lax.rem(me + p, n_exp), me).start()

    half_span = group * fold
    si = lax.broadcasted_iota(jnp.int32, (half_span, span), 0)
    sl = lax.broadcasted_iota(jnp.int32, (half_span, span), 1)
    sel[:, 0:span] = (sl == si).astype(F32).astype(BF)
    sel[:, span:2 * span] = (sl == si + half_span).astype(F32).astype(BF)

    for st in range(2):
        for mat in range(2):
            acc[st, mat] = jnp.zeros(acc.shape[2:], F32)

    weight = scores_ref[...].astype(F32)
    weight = weight / (weight[0:1, :] + weight[1:2, :])
    share = is_first * weight[0:1, :] + is_second * weight[1:2, :]
    for e in range(n_exp):
        for h in range(2):
            cols = slice(h * rows, (h + 1) * rows)
            pick[e, :, cols] = (pick[e, :, cols].astype(F32) * share[e:e + 1, :]).astype(BF)

    def piece(buf, st, i, k):
        px = lax.rem(x + i, NX)
        py = lax.rem(y - signs[st] * k + 2 * NY, NY)
        return buf.at[st, py, pl.ds(pl.multiple_of(px * width, width), width)]

    def arrive(quarter):
        for i in range(group):
            s = quarter * group + i

            @pl.when(s != me)
            def _():
                pltpu.make_async_copy(disp_in.at[s], disp_in.at[s], disp_recv.at[s]).wait()
        packed = disp_in[pl.ds(quarter * group, group)].reshape(half_span, 2 * width)
        low = lax.dot_general(packed, sel[:, 0:span], first_dims, preferred_element_type=F32)
        high = lax.dot_general(packed, sel[:, span:2 * span], first_dims, preferred_element_type=F32)
        return (low[0:width] + high[width:2 * width]).astype(BF)

    def ag_wait(st, i, k):
        ref = piece(x_buf, st, i, k)
        pltpu.make_async_copy(ref, ref, ag_recv.at[st, k, i]).wait()

    def ag_forward(st, i, k):
        ref = piece(x_buf, st, i, k)
        pltpu.make_async_remote_copy(
            src_ref=ref, dst_ref=ref, send_sem=ag_send.at[st], recv_sem=ag_recv.at[st, k + 1, i],
            device_id=at_xy(x, y + signs[st]), device_id_type=MESH).start()

    def side_copy(src, st, step):
        return pltpu.make_async_remote_copy(
            src_ref=src, dst_ref=piece(x_buf, st, 0, 0), send_sem=side_send.at[st],
            recv_sem=ag_recv.at[st, 0, (NX - step) % NX],
            device_id=at_xy(x + step, y), device_id_type=MESH)

    def relay_out(st):
        return pltpu.make_async_remote_copy(
            src_ref=piece(x_buf, st, 0, 0), dst_ref=x_relay.at[st], send_sem=side_send.at[st],
            recv_sem=relay_recv.at[st], device_id=at_xy(x + signs[st], y), device_id_type=MESH)

    def relay_on(st):
        return pltpu.make_async_remote_copy(
            src_ref=x_relay.at[st], dst_ref=piece(x_buf, st, NX - signs[st], 0), send_sem=side_send.at[st],
            recv_sem=ag_recv.at[st, 0, 2], device_id=at_xy(x + signs[st], y), device_id_type=MESH)

    for st in range(2):
        own = piece(x_buf, st, 0, 0)
        own[...] = arrive(2 * parity + st)
        ag_forward(st, 0, 0)
        relay_out(st).start()
    for st in range(2):
        x_side[st] = arrive(2 * (1 - parity) + st)
    side_copy(x_side.at[0], 0, 1).start()
    side_copy(x_side.at[1], 1, 3).start()
    side_copy(x_side.at[1], 1, 1).start()
    side_copy(x_side.at[0], 0, 3).start()
    for st in range(2):
        pltpu.make_async_copy(x_relay.at[st], x_relay.at[st], relay_recv.at[st]).wait()
        relay_on(st).start()
    for n in range(NX):
        for st in range(2):
            i = OUT_ORDER[st][n]
            k = 1 if i == 0 else 0
            ag_wait(st, i, k)
            ag_forward(st, i, k)
    send_gate_up(2)
    send_gate_up(-2)

    def grow(st, mat, k):
        py = lax.rem(y - signs[st] * k + 2 * NY, NY)
        buf = (gate_w, up_w)[mat]
        weights = jnp.concatenate([buf[b, :, py].reshape(feats, half) for b in range(4)], axis=1)
        acc[st, mat] += lax.dot_general(
            x_buf[st, py], weights, (((0,), (0,)), ((), ())), preferred_element_type=F32)

    def turn_down(c, rows_from):
        turned = down_w[rows_from:rows_from + hidden, pl.ds(pl.multiple_of(c * LANES, LANES), LANES)].T
        for h in range(LANES // width):
            block = c * (LANES // width) + h
            xx, yy = block // NY, block % NY
            down_t[yy, pl.ds(pl.multiple_of(xx * width, width), width), rows_from:rows_from + hidden] = (
                turned[h * width:(h + 1) * width, :])

    col_blocks = NX * NY * width // LANES

    @pl.loop(1, NY)
    def _(k):
        for n in range(NX):
            if n == 2:
                @pl.when(k == NY - 1)
                def _():
                    for side, step, src, dst in sides():
                        ref = down_w.at[pl.ds(dst, half)]
                        pltpu.make_async_copy(ref, ref, down_recv.at[side]).wait()

                    @pl.loop(0, col_blocks)
                    def _(c):
                        turn_down(c, hidden)

            for st in range(2):
                i = OUT_ORDER[st][n]
                if i == 0:
                    @pl.when(k < NY - 1)
                    def _():
                        ag_wait(st, i, k + 1)

                    @pl.when(k < NY - 2)
                    def _():
                        ag_forward(st, i, k + 1)
                else:
                    ag_wait(st, i, k)

                    @pl.when(k < NY - 1)
                    def _():
                        ag_forward(st, i, k)

            if n == 0:
                @pl.when(k - 1 <= NY // 2)
                def _():
                    wait_gate_up(1 - k)
            if n == 2:
                @pl.when((k - 1 >= 1) & (k - 1 < NY // 2))
                def _():
                    wait_gate_up(k - 1)
            grow(n // 2, n % 2, k - 1)

        @pl.when(k == 1)
        def _():
            send_gate_up(3)
            send_gate_up(-3)

        @pl.when(k == 2)
        def _():
            send_gate_up(4)
            send_down()

        @pl.when(k <= 4)
        def _():
            for h in range(col_blocks // 4):
                turn_down((k - 1) * (col_blocks // 4) + h, 0)

    def produce(st, k):
        py = lax.rem(y - signs[st] * k + 2 * NY, NY)
        o_buf[st, py] = lax.dot_general(
            down_t[py], hid[st], last_dims, preferred_element_type=F32).astype(BF)

    def rs_forward(st, i, k):
        pltpu.make_async_remote_copy(
            src_ref=piece(o_buf, st, i, k), dst_ref=piece(r_main, st, i, k), send_sem=rs_send.at[st],
            recv_sem=rs_recv.at[st, k - 1, i], device_id=at_xy(x, y - signs[st]), device_id_type=MESH).start()

    def rs_add(st, i, k):
        got = piece(r_main, st, i, k)
        pltpu.make_async_copy(got, got, rs_recv.at[st, k, i]).wait()
        own = piece(o_buf, st, i, k)
        own[...] = (own[...].astype(F32) + got[...].astype(F32)).astype(BF)

    for st in range(2):
        for mat in range(2):
            grow(st, mat, NY - 1)
        gate = acc[st, 0]
        hid[st] = (gate / (1.0 + jnp.exp(-gate)) * acc[st, 1]).astype(BF)
        produce(st, NY - 1)
        for i in BACK_ORDER:
            rs_forward(st, i, NY - 1)
    for st in range(2):
        produce(st, NY - 2)

    @pl.loop(1, NY - 1)
    def _(r):
        k = NY - 1 - r
        for n, i in enumerate(BACK_ORDER):
            for st in range(2):
                rs_add(st, i, k)
                rs_forward(st, i, k)
            if n < 2:
                produce(n, k - 1)

    for i in BACK_ORDER:
        for st in range(2):
            rs_add(st, i, 0)
            if i > 0:
                pltpu.make_async_remote_copy(
                    src_ref=piece(o_buf, st, i, 0), dst_ref=r_turn.at[st, i - 1], send_sem=rs_send.at[st],
                    recv_sem=turn_recv.at[st, i - 1], device_id=at_xy(x + i, y), device_id_type=MESH).start()

    def ret_copy(dest, src):
        return pltpu.make_async_remote_copy(
            src_ref=ret_out.at[dest], dst_ref=ret_in.at[src], send_sem=ret_send, recv_sem=ret_recv.at[src],
            device_id=(dp, dest), device_id_type=MESH)

    def turn_wait(st, i):
        ref = r_turn.at[st, i - 1]
        pltpu.make_async_copy(ref, ref, turn_recv.at[st, i - 1]).wait()
        return r_turn[st, i - 1].astype(F32)

    def give_back(quarter, total):
        total = total.astype(BF)
        none = jnp.zeros((width, span), BF)
        pair = jnp.concatenate(
            [jnp.concatenate([total, none], axis=1), jnp.concatenate([none, total], axis=1)], axis=0)
        packed = lax.dot_general(sel[...], pair, last_dims, preferred_element_type=F32).astype(BF)
        ret_out[pl.ds(quarter * group, group)] = packed.reshape(group, fold, 2 * width)

    for st in range(2):
        give_back(2 * parity + st, piece(o_buf, st, 0, 0)[...].astype(F32) + turn_wait(st, 2))
    for st in range(2):
        give_back(2 * (1 - parity) + st, turn_wait(st, 1) + turn_wait(st, 3))
    for p in far_first:
        ret_copy(lax.rem(me + p, n_exp), me).start()
    ret_in[me] = ret_out[me]

    combined = jnp.zeros((width, rows), F32)
    for q in range(4):
        for e in range(q * group, (q + 1) * group):
            @pl.when(e != me)
            def _():
                pltpu.make_async_copy(ret_in.at[e], ret_in.at[e], ret_recv.at[e]).wait()
        got = ret_in[q * group:(q + 1) * group].reshape(half_span, 2 * width)
        picked = pick[q * group:(q + 1) * group].reshape(half_span, 2 * rows)
        low = lax.dot_general(got, picked[:, 0:rows], first_dims, preferred_element_type=F32)
        high = lax.dot_general(got, picked[:, rows:2 * rows], first_dims, preferred_element_type=F32)
        combined += low[0:width] + high[width:2 * width]
    out_ref[...] = combined.astype(BF)

    def drained(ref, sem):
        pltpu.make_async_copy(ref, ref, sem).wait()

    sent = pl.ds(0, n_exp - 1)
    drained(disp_out.at[sent], disp_send)
    drained(ret_out.at[sent], ret_send)
    drained(gate_w.at[pl.ds(0, 2)], w_send.at[0])
    drained(up_w.at[pl.ds(0, 2)], w_send.at[1])
    drained(down_w.at[own_cols], w_send.at[2])
    for st in range(2):
        drained(x_buf.at[st, 0], side_send.at[st])
        drained(x_buf.at[st, pl.ds(0, NY - 1)], ag_send.at[st])
        drained(o_buf.at[st, pl.ds(0, NY - 1)], rs_send.at[st])
        drained(o_buf.at[st, 0, pl.ds(0, 3 * width)], rs_send.at[st])


def shards(tokens, routes, scores, gate_weight, up_weight, down_weight):
    n_exp = lax.axis_size("expert")
    rows, width = tokens.shape
    _, feats, hidden = gate_weight.shape
    cap = 3 * rows // n_exp
    group = n_exp // 4
    span = group * cap
    split = (NX, NY, width, hidden)
    both = (4, NX, NY, width, hidden // 2)
    pieces = (2, NY, NX * width, span)
    dma = pltpu.SemaphoreType.DMA
    vmem = pl.BlockSpec(memory_space=pltpu.VMEM)
    hbm = pl.BlockSpec(memory_space=pl.ANY)
    return pl.pallas_call(
        moe_kernel,
        out_shape=jax.ShapeDtypeStruct((width, rows), BF),
        in_specs=[vmem, vmem, vmem, hbm, hbm, hbm],
        out_specs=vmem,
        scratch_shapes=[
            pltpu.VMEM(both, BF),
            pltpu.VMEM(both, BF),
            pltpu.VMEM((2 * hidden, feats), BF),
            pltpu.VMEM((NY, NX * width, 2 * hidden), BF),
            pltpu.VMEM((span // 2, 2 * span), BF),
            pltpu.VMEM((n_exp, cap // 2, 2 * width), BF),
            pltpu.VMEM((n_exp, cap // 2, 2 * width), BF),
            pltpu.VMEM((2, width, span), BF),
            pltpu.VMEM((2, width, span), BF),
            pltpu.VMEM(pieces, BF),
            pltpu.VMEM((2, 2, span, 2 * hidden), F32),
            pltpu.VMEM((2, span, 2 * hidden), BF),
            pltpu.VMEM(pieces, BF),
            pltpu.VMEM(pieces, BF),
            pltpu.VMEM((2, NX - 1, width, span), BF),
            pltpu.VMEM((n_exp, cap // 2, 2 * width), BF),
            pltpu.VMEM((n_exp, cap // 2, 2 * width), BF),
            pltpu.VMEM((n_exp, cap // 2, 2 * rows), BF),
            dma((5,)), dma((3,)), dma((2, 2, NY)), dma((2,)), dma, dma((n_exp,)),
            dma((2,)), dma((2,)), dma((2,)), dma((2, NY, NX)),
            dma((2,)), dma((2, NY, NX)), dma((2, NX - 1)), dma, dma((n_exp,)),
        ],
        compiler_params=pltpu.CompilerParams(
            collective_id=0, has_side_effects=True, vmem_limit_bytes=60 * 1024 * 1024),
    )(
        tokens.T, routes.T, scores.T,
        gate_weight[0].reshape(split), up_weight[0].reshape(split), down_weight[0],
    ).T


def solution(mesh):
    return jax.shard_map(
        shards,
        mesh=mesh,
        in_specs=(
            P("expert", "dp"),
            P("expert", None),
            P("expert", None),
            P("expert", None, "dp"),
            P("expert", None, "dp"),
            P("expert", "dp", None),
        ),
        out_specs=P("expert", "dp"),
        check_vma=False,
    )
```

```python
import functools

import jax
import jax.numpy as jnp
from jax import lax
from jax.experimental import pallas as pl
from jax.experimental.pallas import tpu as pltpu
from jax.sharding import PartitionSpec as P

MESH = pl.DeviceIdType.MESH
NX, NY = 4, 8
LANES = 128
BF, F32 = jnp.bfloat16, jnp.float32


OUT_ORDER = ((0, 3, 1, 2), (0, 1, 3, 2))
BACK_ORDER = (2, 1, 3, 0)


def moe_kernel(
    tokens_ref, routes_ref, scores_ref, gate_hbm, up_hbm, down_hbm, out_ref,
    gate_w, up_w, down_w, down_t, sel, disp_out, disp_in,
    x_side, x_relay, x_buf, acc, hid, o_buf, r_main, r_turn, ret_out, ret_in, pick,
    load_sem, w_send, w_recv, down_recv, disp_send, disp_recv, side_send, relay_recv, ag_send, ag_recv,
    rs_send, rs_recv, turn_recv, ret_send, ret_recv,
):
    n_exp = disp_in.shape[0]
    width, rows = tokens_ref.shape
    group = n_exp // 4
    span = x_buf.shape[3]
    fold = span // group // 2
    hidden = gate_hbm.shape[3]
    half = hidden // 2
    feats = NX * width
    dp = lax.axis_index("dp")
    me = lax.axis_index("expert")
    x, y = dp // NY, dp % NY
    parity = x % 2
    signs = (1, -1)

    def at_xy(px, py):
        return (lax.rem(px + NX, NX) * NY + lax.rem(py + NY, NY), me)

    own_cols = pl.ds(0, hidden)
    loads = [
        pltpu.make_async_copy(hbm.at[:, :, :, pl.ds(h * half, half)], buf.at[h], load_sem.at[2 * mat + h])
        for mat, (hbm, buf) in enumerate(((gate_hbm, gate_w), (up_hbm, up_w)))
        for h in range(2)
    ] + [
        pltpu.make_async_copy(down_hbm, down_w.at[own_cols], load_sem.at[4]),
    ]
    for load in loads:
        load.start()

    barrier = pltpu.get_barrier_semaphore()
    for target in (at_xy(x + 1, y), at_xy(x - 1, y), at_xy(x + 2, y), at_xy(x, y + 1), at_xy(x, y - 1)):
        pl.semaphore_signal(barrier, inc=1, device_id=target, device_id_type=MESH)
    for p in range(1, n_exp):
        pl.semaphore_signal(barrier, inc=1, device_id=(dp, lax.rem(me + p, n_exp)), device_id_type=MESH)

    pl.semaphore_wait(barrier, 5 + n_exp - 1)

    def sides():
        return ((0, 1, half, hidden), (1, -1, 0, hidden + half))

    def send_gate_up(back):
        yy = lax.rem(y + back + NY, NY)
        for side, step, src, dst in sides():
            for mat, buf in enumerate((gate_w, up_w)):
                pltpu.make_async_remote_copy(
                    src_ref=buf.at[src // half, :, yy], dst_ref=buf.at[dst // half, :, yy],
                    send_sem=w_send.at[mat], recv_sem=w_recv.at[mat, side, yy],
                    device_id=at_xy(x + step, y), device_id_type=MESH).start()

    def wait_gate_up(back):
        yy = lax.rem(y + back + NY, NY)
        for side, step, src, dst in sides():
            for mat, buf in enumerate((gate_w, up_w)):
                ref = buf.at[dst // half, :, yy]
                pltpu.make_async_copy(ref, ref, w_recv.at[mat, side, yy]).wait()

    def send_down():
        for side, step, src, dst in sides():
            pltpu.make_async_remote_copy(
                src_ref=down_w.at[pl.ds(src, half)], dst_ref=down_w.at[pl.ds(dst, half)],
                send_sem=w_send.at[2], recv_sem=down_recv.at[side],
                device_id=at_xy(x + step, y), device_id_type=MESH).start()

    for load in loads:
        load.wait()
    send_gate_up(0)
    send_gate_up(1)
    send_gate_up(-1)

    first, second = routes_ref[0:1, :], routes_ref[1:2, :]
    expert_at = lax.broadcasted_iota(jnp.int32, (n_exp, rows), 0)
    is_first = (expert_at == first).astype(F32)
    is_second = (expert_at == second).astype(F32)
    earlier_mask = (
        lax.broadcasted_iota(jnp.int32, (rows, rows), 0) < lax.broadcasted_iota(jnp.int32, (rows, rows), 1)
    ).astype(F32).astype(BF)
    named = is_first + is_second
    earlier = jnp.dot(named.astype(BF), earlier_mask, preferred_element_type=F32)
    rank = jnp.where(named > 0.0, earlier, -1.0)

    tok = tokens_ref[...]
    none = jnp.zeros((width, rows), BF)
    tok_pair = jnp.concatenate(
        [jnp.concatenate([tok, none], axis=1), jnp.concatenate([none, tok], axis=1)], axis=0)
    slot_low = lax.broadcasted_iota(jnp.int32, (fold, rows), 0).astype(F32)
    slot_high = (slot_low + fold).astype(BF)
    slot_low = slot_low.astype(BF)
    last_dims = (((1,), (1,)), ((), ()))
    first_dims = (((0,), (0,)), ((), ()))
    for q in range(4):
        for i in range(group):
            e = q * group + i
            of_slot = jnp.tile(jnp.broadcast_to(rank[e:e + 1, :], (16, rows)).astype(BF), (fold // 16, 1))
            pick[e, :, 0:rows] = jnp.where(slot_low == of_slot, 1.0, 0.0).astype(BF)
            pick[e, :, rows:2 * rows] = jnp.where(slot_high == of_slot, 1.0, 0.0).astype(BF)
        picked = pick[q * group:(q + 1) * group].reshape(group * fold, 2 * rows)
        packed = lax.dot_general(picked, tok_pair, last_dims, preferred_element_type=F32).astype(BF)
        disp_out[q * group:(q + 1) * group] = packed.reshape(group, fold, 2 * width)
    disp_in[me] = disp_out[me]

    def disp_copy(dest, src):
        return pltpu.make_async_remote_copy(
            src_ref=disp_out.at[dest], dst_ref=disp_in.at[src], send_sem=disp_send, recv_sem=disp_recv.at[src],
            device_id=(dp, dest), device_id_type=MESH)

    far_first = sorted(range(1, n_exp), key=lambda p: abs(2 * p - n_exp))
    for p in far_first:
        disp_copy(lax.rem(me + p, n_exp), me).start()

    half_span = group * fold
    si = lax.broadcasted_iota(jnp.int32, (half_span, span), 0)
    sl = lax.broadcasted_iota(jnp.int32, (half_span, span), 1)
    sel[:, 0:span] = (sl == si).astype(F32).astype(BF)
    sel[:, span:2 * span] = (sl == si + half_span).astype(F32).astype(BF)

    for st in range(2):
        for mat in range(2):
            acc[st, mat] = jnp.zeros(acc.shape[2:], F32)

    weight = scores_ref[...].astype(F32)
    weight = weight / (weight[0:1, :] + weight[1:2, :])
    share = is_first * weight[0:1, :] + is_second * weight[1:2, :]
    for e in range(n_exp):
        for h in range(2):
            cols = slice(h * rows, (h + 1) * rows)
            pick[e, :, cols] = (pick[e, :, cols].astype(F32) * share[e:e + 1, :]).astype(BF)

    def piece(buf, st, i, k):
        px = lax.rem(x + i, NX)
        py = lax.rem(y - signs[st] * k + 2 * NY, NY)
        return buf.at[st, py, pl.ds(pl.multiple_of(px * width, width), width)]

    def arrive(quarter):
        for i in range(group):
            s = quarter * group + i

            @pl.when(s != me)
            def _():
                pltpu.make_async_copy(disp_in.at[s], disp_in.at[s], disp_recv.at[s]).wait()
        packed = disp_in[pl.ds(quarter * group, group)].reshape(half_span, 2 * width)
        low = lax.dot_general(packed, sel[:, 0:span], first_dims, preferred_element_type=F32)
        high = lax.dot_general(packed, sel[:, span:2 * span], first_dims, preferred_element_type=F32)
        return (low[0:width] + high[width:2 * width]).astype(BF)

    def ag_wait(st, i, k):
        ref = piece(x_buf, st, i, k)
        pltpu.make_async_copy(ref, ref, ag_recv.at[st, k, i]).wait()

    def ag_forward(st, i, k):
        ref = piece(x_buf, st, i, k)
        pltpu.make_async_remote_copy(
            src_ref=ref, dst_ref=ref, send_sem=ag_send.at[st], recv_sem=ag_recv.at[st, k + 1, i],
            device_id=at_xy(x, y + signs[st]), device_id_type=MESH).start()

    def side_copy(src, st, step):
        return pltpu.make_async_remote_copy(
            src_ref=src, dst_ref=piece(x_buf, st, 0, 0), send_sem=side_send.at[st],
            recv_sem=ag_recv.at[st, 0, (NX - step) % NX],
            device_id=at_xy(x + step, y), device_id_type=MESH)

    def relay_out(st):
        return pltpu.make_async_remote_copy(
            src_ref=piece(x_buf, st, 0, 0), dst_ref=x_relay.at[st], send_sem=side_send.at[st],
            recv_sem=relay_recv.at[st], device_id=at_xy(x + signs[st], y), device_id_type=MESH)

    def relay_on(st):
        return pltpu.make_async_remote_copy(
            src_ref=x_relay.at[st], dst_ref=piece(x_buf, st, NX - signs[st], 0), send_sem=side_send.at[st],
            recv_sem=ag_recv.at[st, 0, 2], device_id=at_xy(x + signs[st], y), device_id_type=MESH)

    for st in range(2):
        own = piece(x_buf, st, 0, 0)
        own[...] = arrive(2 * parity + st)
        ag_forward(st, 0, 0)
        relay_out(st).start()
    for st in range(2):
        x_side[st] = arrive(2 * (1 - parity) + st)
    side_copy(x_side.at[0], 0, 1).start()
    side_copy(x_side.at[1], 1, 3).start()
    side_copy(x_side.at[1], 1, 1).start()
    side_copy(x_side.at[0], 0, 3).start()
    for st in range(2):
        pltpu.make_async_copy(x_relay.at[st], x_relay.at[st], relay_recv.at[st]).wait()
        relay_on(st).start()
    send_gate_up(2)
    send_gate_up(-2)
    for n in range(NX):
        for st in range(2):
            i = OUT_ORDER[st][n]
            k = 1 if i == 0 else 0
            ag_wait(st, i, k)
            ag_forward(st, i, k)

    send_gate_up(3)
    send_gate_up(-3)

    def grow(st, mat, k):
        py = lax.rem(y - signs[st] * k + 2 * NY, NY)
        buf = (gate_w, up_w)[mat]
        weights = jnp.concatenate([buf[b, :, py].reshape(feats, half) for b in range(4)], axis=1)
        acc[st, mat] += lax.dot_general(
            x_buf[st, py], weights, (((0,), (0,)), ((), ())), preferred_element_type=F32)

    def turn_down(c, rows_from):
        turned = down_w[rows_from:rows_from + hidden, pl.ds(pl.multiple_of(c * LANES, LANES), LANES)].T
        for h in range(LANES // width):
            block = c * (LANES // width) + h
            xx, yy = block // NY, block % NY
            down_t[yy, pl.ds(pl.multiple_of(xx * width, width), width), rows_from:rows_from + hidden] = (
                turned[h * width:(h + 1) * width, :])

    col_blocks = NX * NY * width // LANES

    @pl.loop(1, NY)
    def _(k):
        for n in range(NX):
            if n == 2:
                @pl.when(k == NY - 1)
                def _():
                    for side, step, src, dst in sides():
                        ref = down_w.at[pl.ds(dst, half)]
                        pltpu.make_async_copy(ref, ref, down_recv.at[side]).wait()

                    @pl.loop(0, col_blocks)
                    def _(c):
                        turn_down(c, hidden)

            for st in range(2):
                i = OUT_ORDER[st][n]
                if i == 0:
                    @pl.when(k < NY - 1)
                    def _():
                        ag_wait(st, i, k + 1)

                    @pl.when(k < NY - 2)
                    def _():
                        ag_forward(st, i, k + 1)
                else:
                    ag_wait(st, i, k)

                    @pl.when(k < NY - 1)
                    def _():
                        ag_forward(st, i, k)

            if n == 0:
                @pl.when(k - 1 <= NY // 2)
                def _():
                    wait_gate_up(1 - k)
            if n == 2:
                @pl.when((k - 1 >= 1) & (k - 1 < NY // 2))
                def _():
                    wait_gate_up(k - 1)
            grow(n // 2, n % 2, k - 1)

        @pl.when(k == 1)
        def _():
            send_gate_up(4)
            send_down()

        @pl.when(k <= 4)
        def _():
            for h in range(col_blocks // 4):
                turn_down((k - 1) * (col_blocks // 4) + h, 0)

    def produce(st, k):
        py = lax.rem(y - signs[st] * k + 2 * NY, NY)
        o_buf[st, py] = lax.dot_general(
            down_t[py], hid[st], last_dims, preferred_element_type=F32).astype(BF)

    def rs_forward(st, i, k):
        pltpu.make_async_remote_copy(
            src_ref=piece(o_buf, st, i, k), dst_ref=piece(r_main, st, i, k), send_sem=rs_send.at[st],
            recv_sem=rs_recv.at[st, k - 1, i], device_id=at_xy(x, y - signs[st]), device_id_type=MESH).start()

    def rs_add(st, i, k):
        got = piece(r_main, st, i, k)
        pltpu.make_async_copy(got, got, rs_recv.at[st, k, i]).wait()
        own = piece(o_buf, st, i, k)
        own[...] = (own[...].astype(F32) + got[...].astype(F32)).astype(BF)

    for st in range(2):
        for mat in range(2):
            grow(st, mat, NY - 1)
        gate = acc[st, 0]
        hid[st] = (gate / (1.0 + jnp.exp(-gate)) * acc[st, 1]).astype(BF)
        produce(st, NY - 1)
        for i in BACK_ORDER:
            rs_forward(st, i, NY - 1)
    for st in range(2):
        produce(st, NY - 2)

    @pl.loop(1, NY - 1)
    def _(r):
        k = NY - 1 - r
        for n, i in enumerate(BACK_ORDER):
            for st in range(2):
                rs_add(st, i, k)
                rs_forward(st, i, k)
            if n < 2:
                produce(n, k - 1)

    for i in BACK_ORDER:
        for st in range(2):
            rs_add(st, i, 0)
            if i > 0:
                pltpu.make_async_remote_copy(
                    src_ref=piece(o_buf, st, i, 0), dst_ref=r_turn.at[st, i - 1], send_sem=rs_send.at[st],
                    recv_sem=turn_recv.at[st, i - 1], device_id=at_xy(x + i, y), device_id_type=MESH).start()

    def ret_copy(dest, src):
        return pltpu.make_async_remote_copy(
            src_ref=ret_out.at[dest], dst_ref=ret_in.at[src], send_sem=ret_send, recv_sem=ret_recv.at[src],
            device_id=(dp, dest), device_id_type=MESH)

    def turn_wait(st, i):
        ref = r_turn.at[st, i - 1]
        pltpu.make_async_copy(ref, ref, turn_recv.at[st, i - 1]).wait()
        return r_turn[st, i - 1].astype(F32)

    def give_back(quarter, total):
        total = total.astype(BF)
        none = jnp.zeros((width, span), BF)
        pair = jnp.concatenate(
            [jnp.concatenate([total, none], axis=1), jnp.concatenate([none, total], axis=1)], axis=0)
        packed = lax.dot_general(sel[...], pair, last_dims, preferred_element_type=F32).astype(BF)
        ret_out[pl.ds(quarter * group, group)] = packed.reshape(group, fold, 2 * width)

    for st in range(2):
        give_back(2 * parity + st, piece(o_buf, st, 0, 0)[...].astype(F32) + turn_wait(st, 2))
    for st in range(2):
        give_back(2 * (1 - parity) + st, turn_wait(st, 1) + turn_wait(st, 3))
    for p in far_first:
        ret_copy(lax.rem(me + p, n_exp), me).start()
    ret_in[me] = ret_out[me]

    combined = jnp.zeros((width, rows), F32)
    for q in range(4):
        for e in range(q * group, (q + 1) * group):
            @pl.when(e != me)
            def _():
                pltpu.make_async_copy(ret_in.at[e], ret_in.at[e], ret_recv.at[e]).wait()
        got = ret_in[q * group:(q + 1) * group].reshape(half_span, 2 * width)
        picked = pick[q * group:(q + 1) * group].reshape(half_span, 2 * rows)
        low = lax.dot_general(got, picked[:, 0:rows], first_dims, preferred_element_type=F32)
        high = lax.dot_general(got, picked[:, rows:2 * rows], first_dims, preferred_element_type=F32)
        combined += low[0:width] + high[width:2 * width]
    out_ref[...] = combined.astype(BF)

    def drained(ref, sem):
        pltpu.make_async_copy(ref, ref, sem).wait()

    sent = pl.ds(0, n_exp - 1)
    drained(disp_out.at[sent], disp_send)
    drained(ret_out.at[sent], ret_send)
    drained(gate_w.at[pl.ds(0, 2)], w_send.at[0])
    drained(up_w.at[pl.ds(0, 2)], w_send.at[1])
    drained(down_w.at[own_cols], w_send.at[2])
    for st in range(2):
        drained(x_buf.at[st, 0], side_send.at[st])
        drained(x_buf.at[st, pl.ds(0, NY - 1)], ag_send.at[st])
        drained(o_buf.at[st, pl.ds(0, NY - 1)], rs_send.at[st])
        drained(o_buf.at[st, 0, pl.ds(0, 3 * width)], rs_send.at[st])


def shards(tokens, routes, scores, gate_weight, up_weight, down_weight):
    n_exp = lax.axis_size("expert")
    rows, width = tokens.shape
    _, feats, hidden = gate_weight.shape
    cap = 3 * rows // n_exp
    group = n_exp // 4
    span = group * cap
    split = (NX, NY, width, hidden)
    both = (4, NX, NY, width, hidden // 2)
    pieces = (2, NY, NX * width, span)
    dma = pltpu.SemaphoreType.DMA
    vmem = pl.BlockSpec(memory_space=pltpu.VMEM)
    hbm = pl.BlockSpec(memory_space=pl.ANY)
    return pl.pallas_call(
        moe_kernel,
        out_shape=jax.ShapeDtypeStruct((width, rows), BF),
        in_specs=[vmem, vmem, vmem, hbm, hbm, hbm],
        out_specs=vmem,
        scratch_shapes=[
            pltpu.VMEM(both, BF),
            pltpu.VMEM(both, BF),
            pltpu.VMEM((2 * hidden, feats), BF),
            pltpu.VMEM((NY, NX * width, 2 * hidden), BF),
            pltpu.VMEM((span // 2, 2 * span), BF),
            pltpu.VMEM((n_exp, cap // 2, 2 * width), BF),
            pltpu.VMEM((n_exp, cap // 2, 2 * width), BF),
            pltpu.VMEM((2, width, span), BF),
            pltpu.VMEM((2, width, span), BF),
            pltpu.VMEM(pieces, BF),
            pltpu.VMEM((2, 2, span, 2 * hidden), F32),
            pltpu.VMEM((2, span, 2 * hidden), BF),
            pltpu.VMEM(pieces, BF),
            pltpu.VMEM(pieces, BF),
            pltpu.VMEM((2, NX - 1, width, span), BF),
            pltpu.VMEM((n_exp, cap // 2, 2 * width), BF),
            pltpu.VMEM((n_exp, cap // 2, 2 * width), BF),
            pltpu.VMEM((n_exp, cap // 2, 2 * rows), BF),
            dma((5,)), dma((3,)), dma((2, 2, NY)), dma((2,)), dma, dma((n_exp,)),
            dma((2,)), dma((2,)), dma((2,)), dma((2, NY, NX)),
            dma((2,)), dma((2, NY, NX)), dma((2, NX - 1)), dma, dma((n_exp,)),
        ],
        compiler_params=pltpu.CompilerParams(
            collective_id=0, has_side_effects=True, vmem_limit_bytes=60 * 1024 * 1024),
    )(
        tokens.T, routes.T, scores.T,
        gate_weight[0].reshape(split), up_weight[0].reshape(split), down_weight[0],
    ).T


def solution(mesh):
    return jax.shard_map(
        shards,
        mesh=mesh,
        in_specs=(
            P("expert", "dp"),
            P("expert", None),
            P("expert", None),
            P("expert", None, "dp"),
            P("expert", None, "dp"),
            P("expert", "dp", None),
        ),
        out_specs=P("expert", "dp"),
        check_vma=False,
    )
```
